256 devices in a mesh: band: 4 (over y_lo, core), grid: 64 (over z, x, y_hi).
Axes of the slice: x: 4, y: 4 (y_hi: 2, y_lo: 2; y = y_hi * 2 + y_lo), z: 8, core: 2. Of those that a mesh axis runs over, the one named last changes fastest.
Arguments:
- orbitals: float32 [128, 64, 128, 128], P('band', 'grid'), may hold values from -8 to 8
- trials: float32 [4, 64, 128, 128], P('band', 'grid'), may hold values from -6 to 6
- owner_group: int32 [4], replicated, may hold values from 0 to 3, as said below
- block_index: int32 [4], replicated, may hold values from 0 to 3, as said below
Outputs:
- exchange_applied: float32 [4, 64, 128, 128], P('band', 'grid')
The draws below stay inside these ranges and needn't reach their ends.
Inputs may be any that keep to these rules, and one draw needn't show every extreme that they name: `owner_group`: no two steps name the same band group. `block_index`: no two steps name the same block.
All inputs are finite; a program needn't handle non-finite values.
Results may differ from the reference program's by a relative error of at most 0.0001.
Values sent between devices are 32-bit elements; how exact they have to be, the bound alone decides.
No kernel may reach another device: no remote copies, remote signals or barrier semaphores. Data moves between devices by JAX's collectives and lax.ppermute only.
A program may use at most 64 MiB of HBM per device.

```python
import math
import jax
import jax.numpy as jnp
from jax import lax

NY = 128
NZ = 128
BLOCK = 8
HELD_DEV = 32
STEPS = 4
NX = 64
NBLOCKS = 4
BANDS = 128
TRIALS = 4
N_BAND = 4


def draw_orbitals(key, part):
    rough = jax.random.normal(key, (BANDS, NX, NY, NZ), jnp.float32)
    return jnp.clip(rough, -8.0, 8.0)


def draw_owner_group(key, part):
    order = jax.random.permutation(jax.random.fold_in(key, 21), jnp.arange(N_BAND, dtype=jnp.int32))
    return order[:STEPS].astype(jnp.int32)


def draw_block_index(key, part):
    order = jax.random.permutation(jax.random.fold_in(key, 37), jnp.arange(NBLOCKS, dtype=jnp.int32))
    return order[:STEPS].astype(jnp.int32)


def block_levels(own_key, extent, shards, smallest, largest):
    def one(axis_at, shards_of):
        heights = jax.random.uniform(jax.random.fold_in(jax.random.fold_in(own_key, 6), axis_at), (shards_of,), jnp.float32, smallest / len(shards), largest / len(shards))
        return jnp.repeat(jnp.exp(heights), extent[axis_at] // shards_of).reshape((-1,) + (1,) * (len(extent) - axis_at - 1))

    gain = one(*shards[0])
    for cut in shards[1:]:
        gain = gain * one(*cut)
    return gain


def scatter_about(stream_key, dims, spread, bound, shards=(), kind=jnp.bfloat16):
    gain = block_levels(stream_key, dims, shards, -0.22, 0.18) if shards else 1.0
    array = jax.random.normal(stream_key, dims, jnp.float32) * spread * gain
    return jnp.minimum(jnp.maximum(array, -bound), bound).astype(kind)


def setup_inputs(seed: int = 0) -> dict:
    key_list = jax.random.split(jax.random.key(seed), 5)
    return {
        "orbitals": draw_orbitals(jax.random.fold_in(key_list[4], 71), 0),
        "trials": scatter_about(key_list[1], (TRIALS, NX, NY, NZ), 1.0, 6.0, ((0, 4), (1, 64)), jnp.float32),
        "owner_group": draw_owner_group(jax.random.fold_in(key_list[4], 71), 0),
        "block_index": draw_block_index(jax.random.fold_in(key_list[4], 71), 0),
    }


def wrapped_squares(length):
    index = jnp.arange(length, dtype=jnp.int32)
    wrapped = jnp.minimum(index, length - index).astype(jnp.float32)
    return wrapped * wrapped

def reference(orbitals, trials, owner_group, block_index):
    kernel_table = 1.0 / (1.0 + wrapped_squares(NX)[:, None, None] + wrapped_squares(NY)[None, :, None] + wrapped_squares(NZ)[None, None, :])
    root_cells = math.sqrt(NX * NY * NZ)
    accumulated = jnp.zeros(trials.shape, jnp.float32)
    for step_index in range(STEPS):
        start = (owner_group[step_index] * HELD_DEV + block_index[step_index] * BLOCK).astype(jnp.int32)
        block_bands = lax.dynamic_slice_in_dim(orbitals, start, BLOCK, 0)

        def apply_one(target):
            density = block_bands * target[None]
            spectrum = jnp.fft.fftn(density, axes=(1, 2, 3))
            potential = jnp.real(jnp.fft.ifftn(spectrum * kernel_table, axes=(1, 2, 3))) * root_cells
            return -lax.optimization_barrier(jnp.sum(potential * block_bands, axis=0)) / BLOCK
        accumulated = accumulated + lax.map(apply_one, trials)
    return accumulated
```

```python
import math

import jax
import jax.numpy as jnp
import ml_dtypes
import numpy as np
from jax import lax
from jax.experimental import pallas as pl
from jax.experimental.pallas import tpu as pltpu
from jax.sharding import Mesh, PartitionSpec as P

BLOCK = 8
NX, NY, NZ = 64, 128, 128
AXES = ("yl", "c", "zh", "z0", "x", "yh")
SIZES = (2, 2, 4, 2, 4, 2)
SPREAD = ("z0", "x", "yh")
FAR = 4
SHARE = 16
ROWS = NY // SHARE
KEEP = BLOCK // FAR
VMEM = 48 << 20


def frequencies(length):
    index = np.arange(length)
    return np.where(index <= length // 2, index, index - length // 2)


def basis(length):
    index = np.arange(length)
    freq = frequencies(length)
    angle = 2.0 * np.pi / length * (freq[:, None] * index[None, :] % length)
    rows = np.where((index <= length // 2)[:, None], np.cos(angle), np.sin(angle))
    scale = np.where((index == 0) | (index == length // 2), 1.0, 2.0) / length
    return rows * np.sqrt(scale)[:, None]


def halves(table):
    high = table.astype(np.float32).astype(ml_dtypes.bfloat16)
    low = (table - high.astype(np.float64)).astype(ml_dtypes.bfloat16)
    return high, low


def right_table(table):
    high, low = halves(table)
    return np.concatenate(
        [np.concatenate([high, low], 1), np.concatenate([high, np.zeros_like(low)], 1)], 0
    )


def left_table(table):
    high, low = halves(table)
    return np.concatenate([high, high, low], 1)


def split(value):
    high = value.astype(jnp.bfloat16)
    low = (value - high.astype(jnp.float32)).astype(jnp.bfloat16)
    return high, low


def times_right(value, table):
    high, low = split(value)
    both = jnp.dot(
        jnp.concatenate([high, low], axis=1), table, preferred_element_type=jnp.float32
    )
    size = both.shape[1] // 2
    return both[:, :size] + both[:, size:]


def times_left(table, value):
    high, low = split(value)
    return jnp.dot(
        table, jnp.concatenate([high, low, high], axis=0), preferred_element_type=jnp.float32
    )


def forward_kernel(trial, own, second, third, fourth, right, left, out):
    for plane in range(trial.shape[0]):
        for slot, bands in enumerate((own, second, third, fourth)):
            pair = jnp.concatenate(
                [trial[plane] * bands[plane, 0], trial[plane] * bands[plane, 1]], axis=0
            )
            pair = times_right(pair, right[...])
            pair = jnp.concatenate([pair[:NY], pair[NY:]], axis=1)
            pair = times_left(left[...], pair)
            for k in range(KEEP):
                out[:, slot * KEEP + k, plane] = pair[:, k * NZ : (k + 1) * NZ].reshape(
                    SHARE, ROWS, NZ
                )


def inverse_kernel(potential, own, second, third, fourth, right, left, out):
    for plane in range(out.shape[0]):
        total = jnp.zeros((NY, NZ), jnp.float32)
        for slot, bands in enumerate((own, second, third, fourth)):
            pair = jnp.concatenate(
                [potential[:, slot * KEEP + k, plane].reshape(NY, NZ) for k in range(KEEP)],
                axis=1,
            )
            pair = times_left(left[...], pair)
            pair = jnp.concatenate([pair[:, :NZ], pair[:, NZ:]], axis=0)
            pair = times_right(pair, right[...])
            total = total + pair[:NY] * bands[plane, 0] + pair[NY:] * bands[plane, 1]
        out[plane] = total * (-math.sqrt(NX * NY * NZ) / BLOCK)


def solve_kernel(near, rest, squares, base, ahead, back, near_out, rest_out):
    bands = near.shape[1]
    for row in range(ROWS):
        kernel = 1.0 / (squares[...] + base[row : row + 1, :])
        kernel = jnp.concatenate([kernel, kernel], axis=1)
        for band in range(0, bands, 2):
            columns = jnp.concatenate(
                [
                    jnp.concatenate(
                        [near[:, b, 0, row, :]]
                        + [rest[:, b, p, row, :] for p in range(FAR - 1)],
                        axis=0,
                    )
                    for b in (band, band + 1)
                ],
                axis=1,
            )
            columns = times_left(ahead[...], columns) * kernel
            columns = times_left(back[...], columns)
            for i in range(2):
                part = columns[:, i * NZ : (i + 1) * NZ]
                near_out[:, band + i, 0, row, :] = part[:SHARE]
                for p in range(FAR - 1):
                    rest_out[:, band + i, p, row, :] = part[(p + 1) * SHARE : (p + 2) * SHARE]


def params():
    return pltpu.CompilerParams(vmem_limit_bytes=VMEM)


def specs(count):
    return [pl.BlockSpec(memory_space=pltpu.VMEM)] * count


def forward(trial, bands, right, left):
    planes = trial.shape[0]
    shape = (SHARE, 4 * KEEP, planes, ROWS, NZ)
    return pl.pallas_call(
        forward_kernel,
        out_shape=jax.ShapeDtypeStruct(shape, jnp.float32),
        in_specs=specs(7),
        out_specs=specs(1)[0],
        compiler_params=params(),
        cost_estimate=pl.CostEstimate(
            flops=planes * 8 * 128 * 128 * 256 * 6, bytes_accessed=planes << 20, transcendentals=0
        ),
        name="forward_planes",
    )(trial, *bands, right, left)


def inverse(potential, bands, right, left):
    planes = potential.shape[2]
    return pl.pallas_call(
        inverse_kernel,
        out_shape=jax.ShapeDtypeStruct((planes, NY, NZ), jnp.float32),
        in_specs=specs(7),
        out_specs=specs(1)[0],
        compiler_params=params(),
        cost_estimate=pl.CostEstimate(
            flops=planes * 8 * 128 * 128 * 256 * 6, bytes_accessed=planes << 20, transcendentals=0
        ),
        name="inverse_planes",
    )(potential, *bands, right, left)


def solve(near, rest, squares, base, ahead, back):
    return pl.pallas_call(
        solve_kernel,
        out_shape=(
            jax.ShapeDtypeStruct(near.shape, jnp.float32),
            jax.ShapeDtypeStruct(rest.shape, jnp.float32),
        ),
        in_specs=specs(6),
        out_specs=tuple(specs(2)),
        compiler_params=params(),
        cost_estimate=pl.CostEstimate(
            flops=8 * 64 * 64 * 1024 * 12, bytes_accessed=4 << 20, transcendentals=0
        ),
        name="solve_columns",
    )(near, rest, squares, base, ahead, back)


def exchange(value):
    return lax.all_to_all(value, SPREAD, 0, 0, tiled=True)


def swap(value, axis):
    return lax.ppermute(value, axis, [(0, 1), (1, 0)])


def all_blocks(own):
    across = swap(own, "yl")
    return own, swap(own, "c"), across, swap(across, "c")


def local(orbitals, trials, owner_group, block_index):
    plane_table = basis(NY)
    column_table = basis(NX)
    right_ahead = jnp.asarray(right_table(plane_table.T))
    left_ahead = jnp.asarray(left_table(plane_table))
    right_back = jnp.asarray(right_table(plane_table))
    left_back = jnp.asarray(left_table(plane_table.T))
    column_ahead = jnp.asarray(left_table(column_table))
    column_back = jnp.asarray(left_table(column_table.T))
    squares = np.broadcast_to((frequencies(NX)[:, None] ** 2), (NX, NZ)).astype(np.float32)
    grid_squares = 1 + frequencies(NY)[:, None] ** 2 + frequencies(NZ)[None, :] ** 2
    base = lax.dynamic_slice_in_dim(
        jnp.asarray(grid_squares.astype(np.float32)), lax.axis_index(SPREAD) * ROWS, ROWS, 0
    )

    group = lax.axis_index(("yl", "c"))
    mine = jnp.sum(jnp.where(owner_group == group, block_index, 0)) * BLOCK
    far = lax.axis_index("zh")

    def bands_for(place):
        start = mine + lax.rem(place + FAR, FAR) * KEEP
        return lax.dynamic_slice_in_dim(orbitals[:, 0], start, KEEP, 0)

    trial = trials[0]
    near_bands = all_blocks(bands_for(far)[None])
    arrived = []
    for step in range(1, FAR):
        packet = jnp.concatenate([bands_for(far - step), trial], axis=0)
        perm = [(i, (i - step) % FAR) for i in range(FAR)]
        arrived.append(lax.ppermute(packet, "zh", perm))
    near = exchange(forward(trial, near_bands, right_ahead, left_ahead))

    rest_bands = all_blocks(jnp.stack([packet[:KEEP] for packet in arrived]))
    rest_trial = jnp.stack([packet[KEEP] for packet in arrived])
    rest = exchange(forward(rest_trial, rest_bands, right_ahead, left_ahead))

    near, rest = solve(
        near, rest, jnp.asarray(squares), base, column_ahead, column_back
    )
    rest = inverse(exchange(rest), rest_bands, right_back, left_back)
    returned = []
    for step in range(1, FAR):
        perm = [(i, (i + step) % FAR) for i in range(FAR)]
        returned.append(lax.ppermute(rest[step - 1], "zh", perm))
    near = inverse(exchange(near), near_bands, right_back, left_back)
    return (near[0] + returned[0] + returned[1] + returned[2])[None, None]


def solution(mesh):
    fine = Mesh(mesh.devices.reshape(SIZES), AXES)
    spec = P(("yl", "c"), ("zh", "z0", "x", "yh"), None, None)
    return jax.shard_map(
        local,
        mesh=fine,
        in_specs=(spec, spec, P(), P()),
        out_specs=spec,
        check_vma=False,
    )
```

```python
import math

import jax
import jax.numpy as jnp
import ml_dtypes
import numpy as np
from jax import lax
from jax.experimental import pallas as pl
from jax.experimental.pallas import tpu as pltpu
from jax.sharding import Mesh, PartitionSpec as P

BLOCK = 8
NX, NY, NZ = 64, 128, 128
AXES = ("yl", "c", "zh", "z0", "x", "yh")
SIZES = (2, 2, 4, 2, 4, 2)
SPREAD = ("z0", "x", "yh")
FAR = 4
SHARE = 16
ROWS = NY // SHARE
KEEP = BLOCK // FAR
VMEM = 16 << 20


def frequencies(length):
    index = np.arange(length)
    return np.where(index <= length // 2, index, index - length // 2)


def basis(length):
    index = np.arange(length)
    freq = frequencies(length)
    angle = 2.0 * np.pi / length * (freq[:, None] * index[None, :] % length)
    rows = np.where((index <= length // 2)[:, None], np.cos(angle), np.sin(angle))
    scale = np.where((index == 0) | (index == length // 2), 1.0, 2.0) / length
    return rows * np.sqrt(scale)[:, None]


def halves(table):
    high = table.astype(np.float32).astype(ml_dtypes.bfloat16)
    low = (table - high.astype(np.float64)).astype(ml_dtypes.bfloat16)
    return high, low


def right_table(table):
    high, low = halves(table)
    return np.concatenate(
        [np.concatenate([high, low], 1), np.concatenate([high, np.zeros_like(low)], 1)], 0
    )


def left_table(table):
    high, low = halves(table)
    return np.concatenate([high, high, low], 1)


def split(value):
    high = value.astype(jnp.bfloat16)
    low = (value - high.astype(jnp.float32)).astype(jnp.bfloat16)
    return high, low


def times_right(value, table):
    high, low = split(value)
    both = jnp.dot(
        jnp.concatenate([high, low], axis=1), table, preferred_element_type=jnp.float32
    )
    size = both.shape[1] // 2
    return both[:, :size] + both[:, size:]


def times_left(table, value):
    high, low = split(value)
    return jnp.dot(
        table, jnp.concatenate([high, low, high], axis=0), preferred_element_type=jnp.float32
    )


def forward_kernel(*refs):
    trials, bands = refs[:FAR], refs[FAR : FAR + 4]
    right, left, out = refs[FAR + 4 :]
    for plane in range(FAR):
        for slot, block in enumerate(bands):
            pair = jnp.concatenate(
                [trials[plane][0] * block[plane, k] for k in range(KEEP)], axis=0
            )
            pair = times_right(pair, right[...])
            pair = jnp.concatenate([pair[:NY], pair[NY:]], axis=1)
            pair = times_left(left[...], pair)
            for k in range(KEEP):
                out[:, slot * KEEP + k, plane] = pair[:, k * NZ : (k + 1) * NZ].reshape(
                    SHARE, ROWS, NZ
                )


def inverse_kernel(potential, own, second, third, fourth, right, left, *outs):
    for plane in range(FAR):
        total = jnp.zeros((NY, NZ), jnp.float32)
        for slot, bands in enumerate((own, second, third, fourth)):
            pair = jnp.concatenate(
                [potential[:, slot * KEEP + k, plane].reshape(NY, NZ) for k in range(KEEP)],
                axis=1,
            )
            pair = times_left(left[...], pair)
            pair = jnp.concatenate([pair[:, :NZ], pair[:, NZ:]], axis=0)
            pair = times_right(pair, right[...])
            total = total + pair[:NY] * bands[plane, 0] + pair[NY:] * bands[plane, 1]
        outs[plane][...] = total * (-math.sqrt(NX * NY * NZ) / BLOCK)


def solve_kernel(spectrum, squares, base, ahead, back, out):
    bands = spectrum.shape[1]
    for row in range(ROWS):
        kernel = 1.0 / (squares[...] + base[row : row + 1, :])
        kernel = jnp.concatenate([kernel, kernel], axis=1)
        for band in range(0, bands, 2):
            columns = jnp.concatenate(
                [
                    jnp.concatenate([spectrum[:, b, p, row, :] for p in range(FAR)], axis=0)
                    for b in (band, band + 1)
                ],
                axis=1,
            )
            columns = times_left(ahead[...], columns) * kernel
            columns = times_left(back[...], columns)
            for i in range(2):
                part = columns[:, i * NZ : (i + 1) * NZ]
                for p in range(FAR):
                    out[:, band + i, p, row, :] = part[p * SHARE : (p + 1) * SHARE]


def params():
    return pltpu.CompilerParams(vmem_limit_bytes=VMEM)


def specs(count):
    return [pl.BlockSpec(memory_space=pltpu.VMEM)] * count


def cost():
    return pl.CostEstimate(
        flops=FAR * 8 * 128 * 128 * 256 * 6, bytes_accessed=4 << 20, transcendentals=0
    )


def forward(trials, bands, right, left):
    shape = (SHARE, 4 * KEEP, FAR, ROWS, NZ)
    return pl.pallas_call(
        forward_kernel,
        out_shape=jax.ShapeDtypeStruct(shape, jnp.float32),
        in_specs=specs(FAR + 6),
        out_specs=specs(1)[0],
        compiler_params=params(),
        cost_estimate=cost(),
        name="forward_planes",
    )(*trials, *bands, right, left)


def inverse(potential, bands, right, left):
    return pl.pallas_call(
        inverse_kernel,
        out_shape=[jax.ShapeDtypeStruct((NY, NZ), jnp.float32)] * FAR,
        in_specs=specs(7),
        out_specs=specs(FAR),
        compiler_params=params(),
        cost_estimate=cost(),
        name="inverse_planes",
    )(potential, *bands, right, left)


def solve(spectrum, squares, base, ahead, back):
    return pl.pallas_call(
        solve_kernel,
        out_shape=jax.ShapeDtypeStruct(spectrum.shape, jnp.float32),
        in_specs=specs(5),
        out_specs=specs(1)[0],
        compiler_params=params(),
        cost_estimate=cost(),
        name="solve_columns",
    )(spectrum, squares, base, ahead, back)


def exchange(value):
    return lax.all_to_all(value, SPREAD, 0, 0, tiled=True)


def swap(value, axis):
    return lax.ppermute(value, axis, [(0, 1), (1, 0)])


def local(orbitals, trials, owner_group, block_index):
    plane_table = basis(NY)
    column_table = basis(NX)
    right_ahead = jnp.asarray(right_table(plane_table.T))
    left_ahead = jnp.asarray(left_table(plane_table))
    right_back = jnp.asarray(right_table(plane_table))
    left_back = jnp.asarray(left_table(plane_table.T))
    column_ahead = jnp.asarray(left_table(column_table))
    column_back = jnp.asarray(left_table(column_table.T))
    squares = np.broadcast_to((frequencies(NX)[:, None] ** 2), (NX, NZ)).astype(np.float32)
    grid_squares = 1 + frequencies(NY)[:, None] ** 2 + frequencies(NZ)[None, :] ** 2
    base = lax.dynamic_slice_in_dim(
        jnp.asarray(grid_squares.astype(np.float32)), lax.axis_index(SPREAD) * ROWS, ROWS, 0
    )

    group = lax.axis_index(("yl", "c"))
    mine = jnp.sum(jnp.where(owner_group == group, block_index, 0)) * BLOCK
    far = lax.axis_index("zh")

    def bands_for(place):
        start = mine + lax.rem(place + FAR, FAR) * KEEP
        return lax.dynamic_slice_in_dim(orbitals[:, 0], start, KEEP, 0)

    trial = trials[0]
    steps = range(1, FAR)
    there = [[(i, (i - step) % FAR) for i in range(FAR)] for step in steps]
    back = [[(i, (i + step) % FAR) for i in range(FAR)] for step in steps]
    own = jnp.stack(
        [bands_for(far)]
        + [lax.ppermute(bands_for(far - step), "zh", there[step - 1]) for step in steps]
    )
    own, trial = lax.optimization_barrier((own, trial))
    across = swap(own, "yl")
    trial_planes = [lax.ppermute(trial, "zh", perm) for perm in there]
    across, trial_planes = lax.optimization_barrier((across, trial_planes))
    bands = (own, swap(own, "c"), across, swap(across, "c"))
    spectrum = forward([trial] + trial_planes, bands, right_ahead, left_ahead)
    spectrum, base = lax.optimization_barrier((spectrum, base))
    spectrum = solve(
        exchange(spectrum), jnp.asarray(squares), base, column_ahead, column_back
    )
    planes = inverse(exchange(spectrum), bands, right_back, left_back)
    total = planes[0]
    for plane, perm in zip(planes[1:], back):
        total = total + lax.ppermute(plane, "zh", perm)
    return total[None, None]


def solution(mesh):
    fine = Mesh(mesh.devices.reshape(SIZES), AXES)
    spec = P(("yl", "c"), ("zh", "z0", "x", "yh"), None, None)
    return jax.shard_map(
        local,
        mesh=fine,
        in_specs=(spec, spec, P(), P()),
        out_specs=spec,
        check_vma=False,
    )
```

```python
import functools
import math

import jax
import jax.numpy as jnp
import ml_dtypes
import numpy as np
from jax import lax
from jax.experimental import pallas as pl
from jax.experimental.pallas import tpu as pltpu
from jax.sharding import Mesh, PartitionSpec as P

BLOCK = 8
NX, NY, NZ = 64, 128, 128
AXES = ("yl", "c", "zh", "z0", "x", "yh")
SIZES = (2, 2, 4, 2, 4, 2)
SPREAD = ("z0", "x", "yh")
FAR = 4
SHARE = 16
ROWS = NY // SHARE
KEEP = BLOCK // FAR
VMEM = 8 << 20


def frequencies(length):
    index = np.arange(length)
    return np.where(index <= length // 2, index, index - length // 2)


def basis(length):
    index = np.arange(length)
    freq = frequencies(length)
    angle = 2.0 * np.pi / length * (freq[:, None] * index[None, :] % length)
    rows = np.where((index <= length // 2)[:, None], np.cos(angle), np.sin(angle))
    scale = np.where((index == 0) | (index == length // 2), 1.0, 2.0) / length
    return rows * np.sqrt(scale)[:, None]


def halves(table):
    high = table.astype(np.float32).astype(ml_dtypes.bfloat16)
    low = (table - high.astype(np.float64)).astype(ml_dtypes.bfloat16)
    return high, low


def right_table(table):
    high, low = halves(table)
    return np.concatenate(
        [np.concatenate([high, low], 1), np.concatenate([high, np.zeros_like(low)], 1)], 0
    )


def left_table(table):
    high, low = halves(table)
    return np.concatenate([np.concatenate([high, high], 1), np.concatenate([low, low], 1)], 0)


def split(value):
    high = value.astype(jnp.bfloat16)
    low = (value - high.astype(jnp.float32)).astype(jnp.bfloat16)
    return high, low


def times_right(value, table):
    high, low = split(value)
    both = jnp.dot(
        jnp.concatenate([high, low], axis=1), table, preferred_element_type=jnp.float32
    )
    size = both.shape[1] // 2
    return both[:, :size] + both[:, size:]


def times_left(table, value):
    high, low = split(value)
    both = jnp.dot(
        table, jnp.concatenate([high, low], axis=0), preferred_element_type=jnp.float32
    )
    size = both.shape[0] // 2
    return both[:size] + both[size:]


def forward_kernel(*refs):
    trials, bands = refs[:FAR], refs[FAR : FAR + 4]
    right, left, out = refs[FAR + 4 :]
    for plane in range(FAR):
        for slot, block in enumerate(bands):
            pair = jnp.concatenate(
                [trials[plane][0] * block[plane, k] for k in range(KEEP)], axis=0
            )
            pair = times_right(pair, right[...])
            pair = jnp.concatenate([pair[:NY], pair[NY:]], axis=1)
            pair = times_left(left[...], pair)
            for k in range(KEEP):
                out[:, (slot * KEEP + k) * FAR + plane] = pair[:, k * NZ : (k + 1) * NZ].reshape(
                    SHARE, ROWS, NZ
                )


def inverse_kernel(first, potential, own, second, third, fourth, right, left, *outs):
    for index, out in enumerate(outs):
        plane = first + index
        total = jnp.zeros((NY, NZ), jnp.float32)
        for slot, bands in enumerate((own, second, third, fourth)):
            pair = jnp.concatenate(
                [
                    potential[:, (slot * KEEP + k) * FAR + plane].reshape(NY, NZ)
                    for k in range(KEEP)
                ],
                axis=1,
            )
            pair = times_left(left[...], pair)
            pair = jnp.concatenate([pair[:, :NZ], pair[:, NZ:]], axis=0)
            pair = times_right(pair, right[...])
            total = total + pair[:NY] * bands[plane, 0] + pair[NY:] * bands[plane, 1]
        out[...] = total * (-math.sqrt(NX * NY * NZ) / BLOCK)


def solve_kernel(spectrum, squares, lanes, ahead, back, out):
    first = (lax.axis_index("z0") * 8 + lax.axis_index("x") * 2 + lax.axis_index("yh")) * ROWS
    for pair in range(0, ROWS, 2):
        kernels = []
        for row in (pair, pair + 1):
            index = first + row
            freq = jnp.where(index <= NY // 2, index, index - NY // 2)
            square = (freq * freq + 1).astype(jnp.float32)
            kernels.append(1.0 / (squares[...] + (lanes[...] + square)))
        kernel = jnp.concatenate(kernels, axis=1)
        kernel = jnp.concatenate([kernel, kernel], axis=0)
        for start in range(0, 4 * KEEP * FAR, 2 * FAR):
            columns = jnp.concatenate(
                [
                    jnp.concatenate(
                        [spectrum[s, start : start + 2 * FAR, row, :] for s in range(SHARE)],
                        axis=0,
                    )
                    for row in (pair, pair + 1)
                ],
                axis=1,
            )
            columns = times_left(ahead[...], columns) * kernel
            columns = times_left(back[...], columns)
            for i in range(2):
                part = columns[:, i * NZ : (i + 1) * NZ]
                for s in range(SHARE):
                    out[s, start : start + 2 * FAR, pair + i, :] = part[
                        s * 2 * FAR : (s + 1) * 2 * FAR
                    ]


def params():
    return pltpu.CompilerParams(vmem_limit_bytes=VMEM)


def specs(count):
    return [pl.BlockSpec(memory_space=pltpu.VMEM)] * count


def cost():
    return pl.CostEstimate(
        flops=FAR * 8 * 128 * 128 * 256 * 6, bytes_accessed=4 << 20, transcendentals=0
    )


def forward(trials, bands, right, left):
    shape = (SHARE, 4 * KEEP * FAR, ROWS, NZ)
    return pl.pallas_call(
        forward_kernel,
        out_shape=jax.ShapeDtypeStruct(shape, jnp.float32),
        in_specs=specs(FAR + 6),
        out_specs=specs(1)[0],
        compiler_params=params(),
        cost_estimate=cost(),
        name="forward_planes",
    )(*trials, *bands, right, left)


def inverse(first, count, potential, bands, right, left):
    return pl.pallas_call(
        functools.partial(inverse_kernel, first),
        out_shape=[jax.ShapeDtypeStruct((NY, NZ), jnp.float32)] * count,
        in_specs=specs(7),
        out_specs=specs(count),
        compiler_params=params(),
        cost_estimate=cost(),
        name="inverse_planes",
    )(potential, *bands, right, left)


def solve(spectrum, squares, lanes, ahead, back):
    return pl.pallas_call(
        solve_kernel,
        out_shape=jax.ShapeDtypeStruct(spectrum.shape, jnp.float32),
        in_specs=specs(5),
        out_specs=specs(1)[0],
        compiler_params=params(),
        cost_estimate=cost(),
        name="solve_columns",
    )(spectrum, squares, lanes, ahead, back)


def exchange(value):
    return lax.all_to_all(value, SPREAD, 0, 0, tiled=True)


def swap(value, axis):
    return lax.ppermute(value, axis, [(0, 1), (1, 0)])


def local(orbitals, trials, owner_group, block_index):
    plane_table = basis(NY)
    column_table = np.einsum(
        "ab,kps->aksbp", np.eye(2), basis(NX).reshape(NX, FAR, SHARE)
    ).reshape(2 * NX, 2 * NX)
    right_ahead = jnp.asarray(right_table(plane_table.T))
    left_ahead = jnp.asarray(left_table(plane_table))
    right_back = jnp.asarray(right_table(plane_table))
    left_back = jnp.asarray(left_table(plane_table.T))
    column_ahead = jnp.asarray(left_table(column_table))
    column_back = jnp.asarray(left_table(column_table.T))
    squares = np.broadcast_to((frequencies(NX)[:, None] ** 2), (NX, NZ)).astype(np.float32)
    lanes = (frequencies(NZ)[None, :] ** 2).astype(np.float32)

    group = lax.axis_index(("yl", "c"))
    mine = jnp.sum(jnp.where(owner_group == group, block_index, 0)) * BLOCK
    far = lax.axis_index("zh")

    def bands_for(place):
        start = mine + lax.rem(place + FAR, FAR) * KEEP
        return lax.dynamic_slice_in_dim(orbitals[:, 0], start, KEEP, 0)

    trial = trials[0]
    steps = range(1, FAR)
    there = [[(i, (i - step) % FAR) for i in range(FAR)] for step in steps]
    back = [[(i, (i + step) % FAR) for i in range(FAR)] for step in steps]
    own = jnp.stack(
        [bands_for(far)]
        + [lax.ppermute(bands_for(far - step), "zh", there[step - 1]) for step in steps]
    )
    own, trial = lax.optimization_barrier((own, trial))
    across = swap(own, "yl")
    trial_planes = [lax.ppermute(trial, "zh", perm) for perm in there]
    across, trial_planes = lax.optimization_barrier((across, trial_planes))
    bands = (own, swap(own, "c"), across, swap(across, "c"))
    spectrum = forward([trial] + trial_planes, bands, right_ahead, left_ahead)
    spectrum = solve(
        exchange(spectrum), jnp.asarray(squares), jnp.asarray(lanes), column_ahead, column_back
    )
    potential = exchange(spectrum)
    planes = inverse(1, FAR - 1, potential, bands, right_back, left_back)
    planes = [lax.ppermute(plane, "zh", perm) for plane, perm in zip(planes, back)]
    total = inverse(0, 1, potential, bands, right_back, left_back)[0]
    return sum(planes, total)[None, None]


def solution(mesh):
    fine = Mesh(mesh.devices.reshape(SIZES), AXES)
    spec = P(("yl", "c"), ("zh", "z0", "x", "yh"), None, None)
    return jax.shard_map(
        local,
        mesh=fine,
        in_specs=(spec, spec, P(), P()),
        out_specs=spec,
        check_vma=False,
    )
```

```python
import functools
import math

import jax
import jax.numpy as jnp
import ml_dtypes
import numpy as np
from jax import lax
from jax.experimental import pallas as pl
from jax.experimental.pallas import tpu as pltpu
from jax.sharding import Mesh, PartitionSpec as P

BLOCK = 8
NX, NY, NZ = 64, 128, 128
AXES = ("yl", "c", "zh", "z0", "x", "yh")
SIZES = (2, 2, 4, 2, 4, 2)
SPREAD = ("yh", "x", "z0")
FAR = 4
SHARE = 16
ROWS = NY // SHARE
KEEP = BLOCK // FAR
VMEM = 8 << 20


def frequencies(length):
    index = np.arange(length)
    return np.where(index <= length // 2, index, index - length // 2)


def basis(length):
    index = np.arange(length)
    freq = frequencies(length)
    angle = 2.0 * np.pi / length * (freq[:, None] * index[None, :] % length)
    rows = np.where((index <= length // 2)[:, None], np.cos(angle), np.sin(angle))
    scale = np.where((index == 0) | (index == length // 2), 1.0, 2.0) / length
    return rows * np.sqrt(scale)[:, None]


def halves(table):
    high = table.astype(np.float32).astype(ml_dtypes.bfloat16)
    low = (table - high.astype(np.float64)).astype(ml_dtypes.bfloat16)
    return high, low


def right_table(table):
    high, low = halves(table)
    return np.concatenate(
        [np.concatenate([high, low], 1), np.concatenate([high, np.zeros_like(low)], 1)], 0
    )


def left_table(table):
    high, low = halves(table)
    return np.concatenate([np.concatenate([high, high], 1), np.concatenate([low, low], 1)], 0)


def split(value):
    high = value.astype(jnp.bfloat16)
    low = (value - high.astype(jnp.float32)).astype(jnp.bfloat16)
    return high, low


def times_right(value, table):
    high, low = split(value)
    both = jnp.dot(
        jnp.concatenate([high, low], axis=1), table, preferred_element_type=jnp.float32
    )
    size = both.shape[1] // 2
    return both[:, :size] + both[:, size:]


def times_left(table, value):
    high, low = split(value)
    both = jnp.dot(
        table, jnp.concatenate([high, low], axis=0), preferred_element_type=jnp.float32
    )
    size = both.shape[0] // 2
    return both[:size] + both[size:]


def forward_kernel(*refs):
    trials, bands = refs[:FAR], refs[FAR : FAR + 4]
    right, left, out = refs[FAR + 4 :]
    for plane in range(FAR):
        for slot, block in enumerate(bands):
            pair = jnp.concatenate(
                [trials[plane][0] * block[plane, k] for k in range(KEEP)], axis=0
            )
            pair = times_right(pair, right[...])
            pair = jnp.concatenate([pair[:NY], pair[NY:]], axis=1)
            pair = times_left(left[...], pair)
            for k in range(KEEP):
                out[:, (slot * KEEP + k) * FAR + plane] = pair[:, k * NZ : (k + 1) * NZ].reshape(
                    SHARE, ROWS, NZ
                )


def inverse_kernel(first, potential, own, second, third, fourth, right, left, *outs):
    for index, out in enumerate(outs):
        plane = first + index
        total = jnp.zeros((NY, NZ), jnp.float32)
        for slot, bands in enumerate((own, second, third, fourth)):
            pair = jnp.concatenate(
                [
                    potential[:, (slot * KEEP + k) * FAR + plane].reshape(NY, NZ)
                    for k in range(KEEP)
                ],
                axis=1,
            )
            pair = times_left(left[...], pair)
            pair = jnp.concatenate([pair[:, :NZ], pair[:, NZ:]], axis=0)
            pair = times_right(pair, right[...])
            total = total + pair[:NY] * bands[plane, 0] + pair[NY:] * bands[plane, 1]
        out[...] = total * (-math.sqrt(NX * NY * NZ) / BLOCK)


def solve_kernel(spectrum, squares, lanes, ahead, back, out):
    first = (lax.axis_index("yh") * 8 + lax.axis_index("x") * 2 + lax.axis_index("z0") * 1) * ROWS
    for pair in range(0, ROWS, 2):
        kernels = []
        for row in (pair, pair + 1):
            index = first + row
            freq = jnp.where(index <= NY // 2, index, index - NY // 2)
            square = (freq * freq + 1).astype(jnp.float32)
            kernels.append(1.0 / (squares[...] + (lanes[...] + square)))
        kernel = jnp.concatenate(kernels, axis=1)
        kernel = jnp.concatenate([kernel, kernel], axis=0)
        for start in range(0, 4 * KEEP * FAR, 2 * FAR):
            columns = jnp.concatenate(
                [
                    jnp.concatenate(
                        [spectrum[s, start : start + 2 * FAR, row, :] for s in range(SHARE)],
                        axis=0,
                    )
                    for row in (pair, pair + 1)
                ],
                axis=1,
            )
            columns = times_left(ahead[...], columns) * kernel
            columns = times_left(back[...], columns)
            for i in range(2):
                part = columns[:, i * NZ : (i + 1) * NZ]
                for s in range(SHARE):
                    out[s, start : start + 2 * FAR, pair + i, :] = part[
                        s * 2 * FAR : (s + 1) * 2 * FAR
                    ]


def params():
    return pltpu.CompilerParams(vmem_limit_bytes=VMEM)


def specs(count):
    return [pl.BlockSpec(memory_space=pltpu.VMEM)] * count


def cost():
    return pl.CostEstimate(
        flops=FAR * 8 * 128 * 128 * 256 * 6, bytes_accessed=4 << 20, transcendentals=0
    )


def forward(trials, bands, right, left):
    shape = (SHARE, 4 * KEEP * FAR, ROWS, NZ)
    return pl.pallas_call(
        forward_kernel,
        out_shape=jax.ShapeDtypeStruct(shape, jnp.float32),
        in_specs=specs(FAR + 6),
        out_specs=specs(1)[0],
        compiler_params=params(),
        cost_estimate=cost(),
        name="forward_planes",
    )(*trials, *bands, right, left)


def inverse(first, count, potential, bands, right, left):
    return pl.pallas_call(
        functools.partial(inverse_kernel, first),
        out_shape=[jax.ShapeDtypeStruct((NY, NZ), jnp.float32)] * count,
        in_specs=specs(7),
        out_specs=specs(count),
        compiler_params=params(),
        cost_estimate=cost(),
        name="inverse_planes",
    )(potential, *bands, right, left)


def solve(spectrum, squares, lanes, ahead, back):
    return pl.pallas_call(
        solve_kernel,
        out_shape=jax.ShapeDtypeStruct(spectrum.shape, jnp.float32),
        in_specs=specs(5),
        out_specs=specs(1)[0],
        compiler_params=params(),
        cost_estimate=cost(),
        name="solve_columns",
    )(spectrum, squares, lanes, ahead, back)


def exchange(value):
    return lax.all_to_all(value, SPREAD, 0, 0, tiled=True)


def swap(value, axis):
    return lax.ppermute(value, axis, [(0, 1), (1, 0)])


def local(orbitals, trials, owner_group, block_index):
    plane_table = basis(NY)
    by_device = basis(NX).reshape(NX, FAR, 2, 4, 2).transpose(0, 1, 4, 3, 2).reshape(NX, FAR, SHARE)
    column_table = np.einsum(
        "ab,kps->aksbp", np.eye(2), by_device
    ).reshape(2 * NX, 2 * NX)
    right_ahead = jnp.asarray(right_table(plane_table.T))
    left_ahead = jnp.asarray(left_table(plane_table))
    right_back = jnp.asarray(right_table(plane_table))
    left_back = jnp.asarray(left_table(plane_table.T))
    column_ahead = jnp.asarray(left_table(column_table))
    column_back = jnp.asarray(left_table(column_table.T))
    squares = np.broadcast_to((frequencies(NX)[:, None] ** 2), (NX, NZ)).astype(np.float32)
    lanes = (frequencies(NZ)[None, :] ** 2).astype(np.float32)

    group = lax.axis_index(("yl", "c"))
    mine = jnp.sum(jnp.where(owner_group == group, block_index, 0)) * BLOCK
    far = lax.axis_index("zh")

    def bands_for(place, mine):
        start = mine + lax.rem(place + FAR, FAR) * KEEP
        return lax.dynamic_slice_in_dim(orbitals[:, 0], start, KEEP, 0)

    trial = trials[0]
    steps = range(1, FAR)
    there = [[(i, (i - step) % FAR) for i in range(FAR)] for step in steps]
    back = [[(i, (i + step) % FAR) for i in range(FAR)] for step in steps]
    middle = bands_for(far - 2, mine)
    mine, middle = lax.optimization_barrier((mine, middle))
    own = jnp.stack(
        [
            bands_for(far, mine),
            lax.ppermute(bands_for(far - 1, mine), "zh", there[0]),
            lax.ppermute(middle, "zh", there[1]),
            lax.ppermute(bands_for(far - 3, mine), "zh", there[2]),
        ]
    )
    own, trial = lax.optimization_barrier((own, trial))
    across = swap(own, "yl")
    trial_planes = [lax.ppermute(trial, "zh", perm) for perm in there]
    across, trial_planes = lax.optimization_barrier((across, trial_planes))
    bands = (own, swap(own, "c"), across, swap(across, "c"))
    spectrum = forward([trial] + trial_planes, bands, right_ahead, left_ahead)
    spectrum = solve(
        exchange(spectrum), jnp.asarray(squares), jnp.asarray(lanes), column_ahead, column_back
    )
    potential = exchange(spectrum)
    planes = inverse(1, FAR - 1, potential, bands, right_back, left_back)
    planes = [lax.ppermute(plane, "zh", perm) for plane, perm in zip(planes, back)]
    total = inverse(0, 1, potential, bands, right_back, left_back)[0]
    return sum(planes, total)[None, None]


def solution(mesh):
    fine = Mesh(mesh.devices.reshape(SIZES), AXES)
    spec = P(("yl", "c"), ("zh", "z0", "x", "yh"), None, None)
    return jax.shard_map(
        local,
        mesh=fine,
        in_specs=(spec, spec, P(), P()),
        out_specs=spec,
        check_vma=False,
    )
```

```python
import functools
import math

import jax
import jax.numpy as jnp
import ml_dtypes
import numpy as np
from jax import lax
from jax.experimental import pallas as pl
from jax.experimental.pallas import tpu as pltpu
from jax.sharding import Mesh, PartitionSpec as P

BLOCK = 8
NX, NY, NZ = 64, 128, 128
AXES = ("yl", "c", "zh", "z0", "x", "yh")
SIZES = (2, 2, 4, 2, 4, 2)
SPREAD = ("x", "yh", "z0")
FAR = 4
SHARE = 16
ROWS = NY // SHARE
KEEP = BLOCK // FAR
VMEM = 8 << 20


def frequencies(length):
    index = np.arange(length)
    return np.where(index <= length // 2, index, index - length // 2)


def basis(length):
    index = np.arange(length)
    freq = frequencies(length)
    angle = 2.0 * np.pi / length * (freq[:, None] * index[None, :] % length)
    rows = np.where((index <= length // 2)[:, None], np.cos(angle), np.sin(angle))
    scale = np.where((index == 0) | (index == length // 2), 1.0, 2.0) / length
    return rows * np.sqrt(scale)[:, None]


def halves(table):
    high = table.astype(np.float32).astype(ml_dtypes.bfloat16)
    low = (table - high.astype(np.float64)).astype(ml_dtypes.bfloat16)
    return high, low


def right_table(table):
    high, low = halves(table)
    return np.concatenate(
        [np.concatenate([high, low], 1), np.concatenate([high, np.zeros_like(low)], 1)], 0
    )


def left_table(table):
    high, low = halves(table)
    return np.concatenate([np.concatenate([high, high], 1), np.concatenate([low, low], 1)], 0)


def split(value):
    high = value.astype(jnp.bfloat16)
    low = (value - high.astype(jnp.float32)).astype(jnp.bfloat16)
    return high, low


def times_right(value, table):
    high, low = split(value)
    both = jnp.dot(
        jnp.concatenate([high, low], axis=1), table, preferred_element_type=jnp.float32
    )
    size = both.shape[1] // 2
    return both[:, :size] + both[:, size:]


def times_left(table, value):
    high, low = split(value)
    both = jnp.dot(
        table, jnp.concatenate([high, low], axis=0), preferred_element_type=jnp.float32
    )
    size = both.shape[0] // 2
    return both[:size] + both[size:]


def forward_kernel(*refs):
    trials, bands = refs[:FAR], refs[FAR : FAR + 4]
    right, left, out = refs[FAR + 4 :]
    for plane in range(FAR):
        for slot, block in enumerate(bands):
            pair = jnp.concatenate(
                [trials[plane][0] * block[plane, k] for k in range(KEEP)], axis=0
            )
            pair = times_right(pair, right[...])
            pair = jnp.concatenate([pair[:NY], pair[NY:]], axis=1)
            pair = times_left(left[...], pair)
            for k in range(KEEP):
                out[:, (slot * KEEP + k) * FAR + plane] = pair[:, k * NZ : (k + 1) * NZ].reshape(
                    SHARE, ROWS, NZ
                )


def inverse_kernel(first, potential, own, second, third, fourth, right, left, *outs):
    for index, out in enumerate(outs):
        plane = first + index
        total = jnp.zeros((NY, NZ), jnp.float32)
        for slot, bands in enumerate((own, second, third, fourth)):
            pair = jnp.concatenate(
                [
                    potential[:, (slot * KEEP + k) * FAR + plane].reshape(NY, NZ)
                    for k in range(KEEP)
                ],
                axis=1,
            )
            pair = times_left(left[...], pair)
            pair = jnp.concatenate([pair[:, :NZ], pair[:, NZ:]], axis=0)
            pair = times_right(pair, right[...])
            total = total + pair[:NY] * bands[plane, 0] + pair[NY:] * bands[plane, 1]
        out[...] = total * (-math.sqrt(NX * NY * NZ) / BLOCK)


def solve_kernel(spectrum, squares, lanes, ahead, back, out):
    first = (lax.axis_index("x") * 4 + lax.axis_index("yh") * 2 + lax.axis_index("z0") * 1) * ROWS
    for pair in range(0, ROWS, 2):
        kernels = []
        for row in (pair, pair + 1):
            index = first + row
            freq = jnp.where(index <= NY // 2, index, index - NY // 2)
            square = (freq * freq + 1).astype(jnp.float32)
            kernels.append(1.0 / (squares[...] + (lanes[...] + square)))
        kernel = jnp.concatenate(kernels, axis=1)
        kernel = jnp.concatenate([kernel, kernel], axis=0)
        for start in range(0, 4 * KEEP * FAR, 2 * FAR):
            columns = jnp.concatenate(
                [
                    jnp.concatenate(
                        [spectrum[s, start : start + 2 * FAR, row, :] for s in range(SHARE)],
                        axis=0,
                    )
                    for row in (pair, pair + 1)
                ],
                axis=1,
            )
            columns = times_left(ahead[...], columns) * kernel
            columns = times_left(back[...], columns)
            for i in range(2):
                part = columns[:, i * NZ : (i + 1) * NZ]
                for s in range(SHARE):
                    out[s, start : start + 2 * FAR, pair + i, :] = part[
                        s * 2 * FAR : (s + 1) * 2 * FAR
                    ]


def params():
    return pltpu.CompilerParams(vmem_limit_bytes=VMEM)


def specs(count):
    return [pl.BlockSpec(memory_space=pltpu.VMEM)] * count


def cost():
    return pl.CostEstimate(
        flops=FAR * 8 * 128 * 128 * 256 * 6, bytes_accessed=4 << 20, transcendentals=0
    )


def forward(trials, bands, right, left):
    shape = (SHARE, 4 * KEEP * FAR, ROWS, NZ)
    return pl.pallas_call(
        forward_kernel,
        out_shape=jax.ShapeDtypeStruct(shape, jnp.float32),
        in_specs=specs(FAR + 6),
        out_specs=specs(1)[0],
        compiler_params=params(),
        cost_estimate=cost(),
        name="forward_planes",
    )(*trials, *bands, right, left)


def inverse(first, count, potential, bands, right, left):
    return pl.pallas_call(
        functools.partial(inverse_kernel, first),
        out_shape=[jax.ShapeDtypeStruct((NY, NZ), jnp.float32)] * count,
        in_specs=specs(7),
        out_specs=specs(count),
        compiler_params=params(),
        cost_estimate=cost(),
        name="inverse_planes",
    )(potential, *bands, right, left)


def solve(spectrum, squares, lanes, ahead, back):
    return pl.pallas_call(
        solve_kernel,
        out_shape=jax.ShapeDtypeStruct(spectrum.shape, jnp.float32),
        in_specs=specs(5),
        out_specs=specs(1)[0],
        compiler_params=params(),
        cost_estimate=cost(),
        name="solve_columns",
    )(spectrum, squares, lanes, ahead, back)


def exchange(value):
    return lax.all_to_all(value, SPREAD, 0, 0, tiled=True)


def swap(value, axis):
    return lax.ppermute(value, axis, [(0, 1), (1, 0)])


def local(orbitals, trials, owner_group, block_index):
    plane_table = basis(NY)
    by_device = basis(NX).reshape(NX, FAR, 2, 4, 2).transpose(0, 1, 3, 4, 2).reshape(NX, FAR, SHARE)
    column_table = np.einsum(
        "ab,kps->aksbp", np.eye(2), by_device
    ).reshape(2 * NX, 2 * NX)
    right_ahead = jnp.asarray(right_table(plane_table.T))
    left_ahead = jnp.asarray(left_table(plane_table))
    right_back = jnp.asarray(right_table(plane_table))
    left_back = jnp.asarray(left_table(plane_table.T))
    column_ahead = jnp.asarray(left_table(column_table))
    column_back = jnp.asarray(left_table(column_table.T))
    squares = np.broadcast_to((frequencies(NX)[:, None] ** 2), (NX, NZ)).astype(np.float32)
    lanes = (frequencies(NZ)[None, :] ** 2).astype(np.float32)

    group = lax.axis_index(("yl", "c"))
    mine = jnp.sum(jnp.where(owner_group == group, block_index, 0)) * BLOCK
    far = lax.axis_index("zh")

    def bands_for(place, mine):
        start = mine + lax.rem(place + FAR, FAR) * KEEP
        return lax.dynamic_slice_in_dim(orbitals[:, 0], start, KEEP, 0)

    trial = trials[0]
    steps = range(1, FAR)
    there = [[(i, (i - step) % FAR) for i in range(FAR)] for step in steps]
    back = [[(i, (i + step) % FAR) for i in range(FAR)] for step in steps]
    middle = bands_for(far - 2, mine)
    mine, middle = lax.optimization_barrier((mine, middle))
    own = jnp.stack(
        [
            bands_for(far, mine),
            lax.ppermute(bands_for(far - 1, mine), "zh", there[0]),
            lax.ppermute(middle, "zh", there[1]),
            lax.ppermute(bands_for(far - 3, mine), "zh", there[2]),
        ]
    )
    own, trial = lax.optimization_barrier((own, trial))
    across = swap(own, "yl")
    trial_planes = [lax.ppermute(trial, "zh", perm) for perm in there]
    across, trial_planes = lax.optimization_barrier((across, trial_planes))
    bands = (own, swap(own, "c"), across, swap(across, "c"))
    spectrum = forward([trial] + trial_planes, bands, right_ahead, left_ahead)
    spectrum = solve(
        exchange(spectrum), jnp.asarray(squares), jnp.asarray(lanes), column_ahead, column_back
    )
    potential = exchange(spectrum)
    planes = inverse(1, FAR - 1, potential, bands, right_back, left_back)
    planes = [lax.ppermute(plane, "zh", perm) for plane, perm in zip(planes, back)]
    total = inverse(0, 1, potential, bands, right_back, left_back)[0]
    return sum(planes, total)[None, None]


def solution(mesh):
    fine = Mesh(mesh.devices.reshape(SIZES), AXES)
    spec = P(("yl", "c"), ("zh", "z0", "x", "yh"), None, None)
    return jax.shard_map(
        local,
        mesh=fine,
        in_specs=(spec, spec, P(), P()),
        out_specs=spec,
        check_vma=False,
    )
```
